32 devices in a mesh: dp: 8 (over z, y), tensor: 4 (over x, core).
Axes of the slice: x: 2, y: 2, z: 4, core: 2. Of those that a mesh axis runs over, the one named last changes fastest.
Arguments:
- query: bfloat16 [64, 64, 128], P('dp', 'tensor'), may hold values from -8 to 8
- kv_pages: bfloat16 [560, 8, 2, 128, 128], P('dp', 'tensor'), may hold values from -8 to 8
- move_plan: int32 [8, 3, 12], P('dp'), may hold values from 0 to 69, as said below
- move_count: int32 [8], P('dp'), may hold values from 9 to 12
- block_table: int32 [64, 8], P('dp'), may hold values from 0 to 69, as said below
- seq_lens: int32 [64], P('dp'), may hold values from 1 to 1024
- out_weight: bfloat16 [8192, 8192], P('tensor', 'dp'), may hold values from -0.0625 to 0.0625
Outputs:
- new_pages: bfloat16 [560, 8, 2, 128, 128], P('dp', 'tensor')
- projected: bfloat16 [64, 8192], P(None, 'dp')
The draws below stay inside these ranges and needn't reach their ends.
Inputs may be any that keep to these rules, and one draw needn't show every extreme that they name: `move_plan`: row 0 holds the device's own source slots, distinct within a device; row 1 target devices; row 2 target slots. Entries at or past the device's move_count are padding to be ignored. At most 2 valid moves go from one device to one device, and some pair has exactly 2. The (target device, target slot) pairs of all valid moves are distinct. `block_table`: all entries of the sequences of one device are distinct slots of that device; sequence s belongs to device s // 8.
All inputs are finite; a program needn't handle non-finite values.
Results may differ from the reference program's by a relative error of at most 0.0055.
Values may be sent and summed in bfloat16 or wider, within the bound.
No kernel may reach another device: no remote copies, remote signals or barrier semaphores. Data moves between devices by JAX's collectives and lax.ppermute only.
A program may use at most 128 MiB of HBM per device.

```python
import math
import jax
import jax.numpy as jnp
from jax import lax

D = 8192
HQ = 64
KVH = 8
HD = 128
BLOCK = 128
BLOCKS = 8
CAP = 2
SEQ_DEV = 8
MOVES = 12
SLOTS = 70
SEQS = 64
TOTAL_SLOTS = 560
N_DP = 8


def derive(key, number):
    return jax.random.fold_in(key, number)


def move_layout(key):
    frequent_pages = jax.random.permutation(derive(key, 101), N_DP)[:2]
    extra_increment = jnp.zeros((N_DP,), jnp.int32).at[frequent_pages].set(2 ** 19)
    random_perturbation = jax.random.randint(derive(key, 102), (N_DP, N_DP), 0, 2 ** 20)
    order_ranks = (random_perturbation + extra_increment[None, :]) * N_DP + jnp.arange(N_DP, dtype=jnp.int32)[None, :]
    chosen = jnp.argsort(-order_ranks, axis=1, stable=True)[:, :MOVES // CAP]
    target_dev = jnp.repeat(chosen, CAP, axis=1).astype(jnp.int32)
    live_moves = jax.random.randint(derive(key, 103), (N_DP,), 3 * MOVES // 4, MOVES + 1).astype(jnp.int32)
    is_valid = jnp.arange(MOVES, dtype=jnp.int32)[None, :] < live_moves[:, None]
    slot_index = jnp.arange(SLOTS, dtype=jnp.int32)[None, :]
    source_key = jax.random.randint(derive(key, 104), (N_DP, SLOTS), 0, 2 ** 20) * SLOTS + slot_index
    source_slot = jnp.argsort(source_key, axis=1, stable=True)[:, :MOVES].astype(jnp.int32)
    shuffle_key = jax.random.randint(derive(key, 105), (N_DP, SLOTS), 0, 2 ** 20) * SLOTS + slot_index
    shuffled = jnp.argsort(shuffle_key, axis=1, stable=True).astype(jnp.int32)
    external_pages = (slot_index >= SEQ_DEV * BLOCKS).astype(jnp.int32)
    priority = (jax.random.randint(derive(key, 106), (N_DP, SLOTS), 0, 2 ** 20) + external_pages * 2 ** 21) * SLOTS + slot_index
    fill_order = jnp.argsort(priority, axis=1, stable=True)
    target_list = jnp.take_along_axis(shuffled, fill_order, axis=1)
    flat_dev = target_dev.reshape(-1)
    onehot = ((flat_dev[:, None] == jnp.arange(N_DP, dtype=jnp.int32)[None, :]) & is_valid.reshape(-1)[:, None]).astype(jnp.int32)
    before = jnp.cumsum(onehot, axis=0) - onehot
    dest_rank = jnp.sum(before * onehot, axis=1)
    target_slot = target_list[flat_dev, dest_rank].reshape(N_DP, MOVES)
    filler = jax.random.randint(derive(key, 107), (N_DP, MOVES), 0, SLOTS).astype(jnp.int32)
    target_slot = jnp.where(is_valid, target_slot, filler)
    move_plan = jnp.stack([source_slot, target_dev, target_slot], axis=1).astype(jnp.int32)
    page_table = shuffled[:, :SEQ_DEV * BLOCKS].reshape(N_DP * SEQ_DEV, BLOCKS).astype(jnp.int32)
    return (move_plan, live_moves, page_table)


def draw_move_plan(key, part):
    return move_layout(key)[0]


def draw_move_count(key, part):
    return move_layout(key)[1]


def draw_block_table(key, part):
    return move_layout(key)[2]


def draw_query(key, part):
    shape = (SEQS, HQ, HD)
    values = jnp.clip(jax.random.normal(derive(key, 14), shape, jnp.float32), -6.0, 6.0)
    return values.astype(jnp.bfloat16)


def draw_kv_pages(key, part):
    shape = (TOTAL_SLOTS, KVH, 2, BLOCK, HD)
    values = jnp.clip(jax.random.normal(derive(key, 24), shape, jnp.float32), -6.0, 6.0)
    return values.astype(jnp.bfloat16)


def set_ends(entries, rng, smallest, high):
    place = [jax.random.randint(jax.random.fold_in(rng, axis), (), 0, length) for axis, length in enumerate(entries.shape)]
    widest = entries.shape.index(max(entries.shape))
    next_to = place[:widest] + [(place[widest] + 1) % entries.shape[widest]] + place[widest + 1:]
    return entries.at[tuple(place)].set(smallest).at[tuple(next_to)].set(high)


def level_of(rng, extent, shards, least, top_value):
    factor_of = 1.0
    for axis_at, blocks in shards:
        heights = jax.random.uniform(jax.random.fold_in(jax.random.fold_in(rng, 6), axis_at), (blocks,), jnp.float32, least / len(shards), top_value / len(shards))
        factor_of = factor_of * jnp.repeat(jnp.exp(heights), extent[axis_at] // blocks).reshape((-1,) + (1,) * (len(extent) - 1 - axis_at))
    return factor_of


def normal_values(rng, shape, scale, most, split=(), kind=jnp.bfloat16):
    drawn = jax.random.normal(rng, shape, jnp.float32) * scale
    if len(split) > 0:
        drawn = level_of(rng, shape, split, -0.22, 0.18) * drawn
    return jnp.clip(drawn, min=-most, max=most).astype(kind)


def setup_inputs(seed: int = 0) -> dict:
    key_list = jax.random.split(jax.random.key(seed), 8)
    return {
        "query": draw_query(jax.random.fold_in(key_list[7], 71), 0),
        "kv_pages": draw_kv_pages(jax.random.fold_in(key_list[7], 71), 0),
        "move_plan": draw_move_plan(jax.random.fold_in(key_list[7], 71), 0),
        "move_count": draw_move_count(jax.random.fold_in(key_list[7], 71), 0),
        "block_table": draw_block_table(jax.random.fold_in(key_list[7], 71), 0),
        "seq_lens": set_ends(jax.random.randint(key_list[5], (SEQS,), 1, BLOCKS * BLOCK + 1), jax.random.fold_in(key_list[5], 1), 1, BLOCKS * BLOCK).astype(jnp.int32),
        "out_weight": normal_values(key_list[6], (HQ * HD, D), (HQ * HD) ** -0.5, 0.0625, ((0, 4), (1, 8))),
    }


def reference(query, kv_pages, move_plan, move_count, block_table, seq_lens, out_weight):
    sender = jnp.arange(N_DP, dtype=jnp.int32)[:, None]
    is_valid = jnp.arange(MOVES, dtype=jnp.int32)[None, :] < move_count[:, None]
    source = (sender * SLOTS + move_plan[:, 0, :]).reshape(-1).astype(jnp.int32)
    target = jnp.where(is_valid, move_plan[:, 1, :] * SLOTS + move_plan[:, 2, :], TOTAL_SLOTS)
    target = target.reshape(-1).astype(jnp.int32)
    new_pages = kv_pages.at[target].set(kv_pages[source], mode='drop')
    owner_dev = jnp.arange(SEQS, dtype=jnp.int32) // SEQ_DEV
    page_slots = (owner_dev[:, None] * SLOTS + block_table).astype(jnp.int32)
    position = jnp.arange(BLOCKS * BLOCK, dtype=jnp.int32)
    score_scale = 1.0 / math.sqrt(HD)

    def attend(inputs):
        query_row, rows_used, length = inputs
        gathered = new_pages[rows_used]
        key_rows = jnp.transpose(gathered[:, :, 0], (1, 0, 2, 3)).reshape(KVH, BLOCKS * BLOCK, HD).astype(jnp.float32)
        value_rows = jnp.transpose(gathered[:, :, 1], (1, 0, 2, 3)).reshape(KVH, BLOCKS * BLOCK, HD).astype(jnp.float32)
        grouped = query_row.reshape(KVH, HQ // KVH, HD).astype(jnp.float32)
        scores = jnp.einsum('kgd,ktd->kgt', grouped, key_rows) * score_scale
        scores = jnp.where(position[None, None, :] < length, scores, -1e+30)
        largest = lax.optimization_barrier(jnp.max(scores, axis=-1, keepdims=True))
        expo = jnp.exp(scores - largest)
        weights = (expo / lax.optimization_barrier(jnp.sum(expo, axis=-1, keepdims=True))).astype(jnp.bfloat16)
        mixed_heads = jnp.einsum('kgt,ktd->kgd', weights.astype(jnp.float32), value_rows)
        return mixed_heads.reshape(HQ * HD).astype(jnp.bfloat16)
    attention = lax.map(attend, (query, page_slots, seq_lens))
    projected = jnp.dot(attention, out_weight, preferred_element_type=jnp.float32).astype(jnp.bfloat16)
    return (new_pages, projected)
```

```python
import functools
import math

import jax
import jax.numpy as jnp
from jax import lax
from jax.experimental import pallas as pl
from jax.experimental.pallas import tpu as pltpu
from jax.sharding import PartitionSpec as P

CAP = 2
ROW = 8
NEG = -1e30

ANY = pl.BlockSpec(memory_space=pl.ANY)
VMEM = pl.BlockSpec(memory_space=pltpu.VMEM)
SMEM = pl.BlockSpec(memory_space=pltpu.SMEM)


def pack_kernel(plan, count, pages, out, used, tags, sem):
    devices = out.shape[0]
    rows = pages.shape[1]
    moves = plan.shape[1]
    for d in range(devices):
        used[d] = 0
        for r in range(CAP):
            tags[d * CAP + r] = -1

    def page_copy(source, target, rank):
        place = pl.ds(pl.multiple_of(rank * rows, rows), rows)
        return pltpu.make_async_copy(pages.at[source], out.at[target, place], sem)

    def send(k, carry):
        @pl.when(k < count[0])
        def _():
            target = plan[1, k]
            rank = used[target]
            used[target] = rank + 1
            tags[target * CAP + rank] = plan[2, k]
            page_copy(plan[0, k], target, rank).start()

        return carry

    lax.fori_loop(0, moves, send, 0)
    row_at = lax.broadcasted_iota(jnp.int32, (ROW, pages.shape[2]), 0)
    for d in range(devices):
        tile = jnp.full(row_at.shape, -1, jnp.int32)
        for r in range(CAP):
            tile = jnp.where(row_at == r, tags[d * CAP + r], tile)
        out[d, CAP * rows :] = tile.astype(jnp.float32).astype(out.dtype)

    def finish(k, carry):
        @pl.when(k < count[0])
        def _():
            page_copy(0, 0, 0).wait()

        return carry

    lax.fori_loop(0, moves, finish, 0)


def page_partial(q8, key_page, value_page, first, length, scale):
    scores = (
        lax.dot_general(
            q8, key_page, (((1,), (1,)), ((), ())), preferred_element_type=jnp.float32
        )
        * scale
    )
    position = first + lax.broadcasted_iota(jnp.int32, scores.shape, 1)
    scores = jnp.where(position < length, scores, NEG)
    largest = jnp.max(scores, axis=1, keepdims=True)
    expo = jnp.exp(scores - largest)
    total = jnp.sum(expo, axis=1, keepdims=True)
    mixed = jnp.dot(
        expo.astype(jnp.bfloat16), value_page, preferred_element_type=jnp.float32
    )
    return largest, total, mixed


def local_kernel(
    heads, scale, table, lens, query, pages, new_pages, mixed_out, stat_out, owner,
    held, read_sem, write_sem,
):
    slots = pages.shape[0]
    block = pages.shape[1] // (2 * heads)
    seqs, blocks = table.shape
    group = query.shape[1] // heads
    lanes = query.shape[2]

    def read(i):
        return pltpu.make_async_copy(pages.at[i], held.at[i], read_sem.at[i])

    def write(i):
        return pltpu.make_async_copy(held.at[i], new_pages.at[i], write_sem)

    def start_read(i, carry):
        read(i).start()
        owner[i] = -1
        return carry

    lax.fori_loop(0, slots, start_read, 0)

    def own(i, carry):
        for b in range(blocks):
            owner[table[i, b]] = i * blocks + b
        return carry

    lax.fori_loop(0, seqs, own, 0)

    def pass_on(i, carry):
        read(i).wait()
        write(i).start()
        return carry

    lax.fori_loop(0, slots, pass_on, 0)
    lane_at = lax.broadcasted_iota(jnp.int32, (group, lanes), 1)

    def sequence(i, carry):
        length = lens[i]
        q_rows = query[i].astype(jnp.float32)
        for b in range(blocks):
            slot = table[i, b]
            for h in range(heads):
                q8 = q_rows[h * group : (h + 1) * group].astype(jnp.bfloat16)
                top = 2 * h * block
                largest, total, mixed = page_partial(
                    q8,
                    held[slot, top : top + block],
                    held[slot, top + block : top + 2 * block],
                    b * block,
                    length,
                    scale,
                )
                mixed_out[i, b, h] = mixed
                stat_out[i, b, h] = jnp.where(lane_at < lanes // 2, largest, total)
        return carry

    lax.fori_loop(0, seqs, sequence, 0)

    def finish(i, carry):
        write(i).wait()
        return carry

    lax.fori_loop(0, slots, finish, 0)


def final_kernel(
    heads, scale, copies, lens, owner, query, arrived, mixed_in, stat_in, pages_in,
    pages_out, out, mixed, stat, tags, sem, in_sem,
):
    devices = arrived.shape[0]
    rows = pages_out.shape[1]
    block = rows // (2 * heads)
    seqs = query.shape[0]
    blocks = mixed_in.shape[1]
    group = query.shape[1] // heads
    lanes = query.shape[2]
    fetch = [
        pltpu.make_async_copy(mixed_in, mixed, in_sem.at[0]),
        pltpu.make_async_copy(stat_in, stat, in_sem.at[1]),
    ]
    for copy in fetch:
        copy.start()

    row_at = lax.broadcasted_iota(jnp.int32, (ROW, lanes), 0)
    for d in range(devices):
        tile = arrived[d, CAP * rows :].astype(jnp.float32)
        for r in range(CAP):
            tags[d * CAP + r] = jnp.max(jnp.where(row_at == r, tile, -1.0)).astype(jnp.int32)

    def place(d, r, slot):
        return pltpu.make_async_copy(
            arrived.at[d, pl.ds(r * rows, rows)], pages_out.at[slot], sem
        )

    for d in range(devices):
        for r in range(CAP):
            @pl.when(tags[d * CAP + r] >= 0)
            def _():
                place(d, r, tags[d * CAP + r]).start()

    for copy in fetch:
        copy.wait()
    lane_at = lax.broadcasted_iota(jnp.int32, (group, lanes), 1)

    def renew(d):
        for r in range(CAP):
            slot = tags[d * CAP + r]
            entry = jnp.where(slot >= 0, owner[jnp.maximum(slot, 0)], -1)
            at = jnp.maximum(entry, 0)
            i = at // blocks
            b = at - i * blocks
            q_rows = query[i].astype(jnp.float32)
            found = []
            for h in range(heads):
                q8 = q_rows[h * group : (h + 1) * group].astype(jnp.bfloat16)
                top = r * rows + 2 * h * block
                found.append(
                    page_partial(
                        q8,
                        arrived[d, top : top + block],
                        arrived[d, top + block : top + 2 * block],
                        b * block,
                        lens[i],
                        scale,
                    )
                )

            @pl.when(entry >= 0)
            def _():
                for h, (largest, total, part) in enumerate(found):
                    mixed[i, b, h] = part
                    stat[i, b, h] = jnp.where(lane_at < lanes // 2, largest, total)

    if devices <= 8:
        for d in range(devices):
            renew(d)
    else:
        lax.fori_loop(0, devices, lambda d, c: (renew(d), c)[1], 0)

    for h in range(heads):
        for i in range(seqs):
            stats = stat[i, :, h]
            largest = stats[:, :, :1]
            total = stats[:, :, lanes // 2 : lanes // 2 + 1]
            top = jnp.max(largest, axis=0, keepdims=True)
            factor = jnp.exp(largest - top)
            weight = factor / jnp.sum(factor * total, axis=0, keepdims=True)
            value = jnp.sum(mixed[i, :, h] * weight, axis=0).astype(out.dtype)
            for c in range(copies):
                out[c, i, h * group : (h + 1) * group] = value

    for d in range(devices):
        for r in range(CAP):
            @pl.when(tags[d * CAP + r] >= 0)
            def _():
                place(d, r, 0).wait()


def exchange_sum(value, size):
    me = lax.axis_index("tensor")
    pairs = lambda bit: [(i, i ^ bit) for i in range(size)]
    half = value.shape[0] // 2
    low = (me % 2) == 0
    travel = value.astype(jnp.bfloat16)
    given = jnp.where(low, travel[half:], travel[:half])
    kept = jnp.where(low, value[:half], value[half:])
    total = kept + lax.ppermute(given, "tensor", pairs(1)).astype(jnp.float32)
    bit = 2
    while bit < size:
        total = total + lax.ppermute(
            total.astype(jnp.bfloat16), "tensor", pairs(bit)
        ).astype(jnp.float32)
        bit *= 2
    mine = total.astype(jnp.bfloat16)
    other = lax.ppermute(mine, "tensor", pairs(1))
    return jnp.concatenate([jnp.where(low, mine, other), jnp.where(low, other, mine)])


def body(query, kv_pages, move_plan, move_count, block_table, seq_lens, out_weight):
    slots, heads, two, block, lanes = kv_pages.shape
    seqs, local_q, _ = query.shape
    devices = lax.axis_size("dp")
    tensor = lax.axis_size("tensor")
    blocks = block_table.shape[1]
    group = local_q // heads
    rows = heads * two * block
    scale = 1.0 / math.sqrt(lanes)
    pages = kv_pages.reshape(slots, rows, lanes)
    plan = move_plan.reshape(move_plan.shape[1:])

    outgoing = pl.pallas_call(
        pack_kernel,
        out_shape=jax.ShapeDtypeStruct((devices, CAP * rows + ROW, lanes), kv_pages.dtype),
        in_specs=[SMEM, SMEM, ANY],
        out_specs=VMEM,
        scratch_shapes=[
            pltpu.SMEM((devices,), jnp.int32),
            pltpu.SMEM((devices * CAP,), jnp.int32),
            pltpu.SemaphoreType.DMA,
        ],
        name="pack",
    )(plan, move_count, pages)
    arrived = lax.all_to_all(outgoing, "dp", split_axis=0, concat_axis=0, tiled=True)

    part_shape = jax.ShapeDtypeStruct((seqs, blocks, heads, group, lanes), jnp.float32)
    copied, mixed, stat, owner = pl.pallas_call(
        functools.partial(local_kernel, heads, scale),
        out_shape=(
            jax.ShapeDtypeStruct(pages.shape, pages.dtype),
            part_shape,
            part_shape,
            jax.ShapeDtypeStruct((slots,), jnp.int32),
        ),
        in_specs=[SMEM, SMEM, VMEM, ANY],
        out_specs=(ANY, VMEM, VMEM, SMEM),
        scratch_shapes=[
            pltpu.VMEM(pages.shape, pages.dtype),
            pltpu.SemaphoreType.DMA((slots,)),
            pltpu.SemaphoreType.DMA,
        ],
        name="local",
        cost_estimate=pl.CostEstimate(
            flops=4 * seqs * blocks * local_q * block * lanes,
            bytes_accessed=4 * slots * rows * lanes,
            transcendentals=0,
        ),
    )(block_table, seq_lens, query, pages)

    new_pages, attention = pl.pallas_call(
        functools.partial(final_kernel, heads, scale, devices),
        out_shape=(
            jax.ShapeDtypeStruct(pages.shape, pages.dtype),
            jax.ShapeDtypeStruct((devices, seqs, local_q, lanes), jnp.bfloat16),
        ),
        in_specs=[SMEM, SMEM, VMEM, VMEM, ANY, ANY, ANY],
        out_specs=(ANY, VMEM),
        scratch_shapes=[
            pltpu.VMEM(part_shape.shape, jnp.float32),
            pltpu.VMEM(part_shape.shape, jnp.float32),
            pltpu.SMEM((devices * CAP,), jnp.int32),
            pltpu.SemaphoreType.DMA,
            pltpu.SemaphoreType.DMA((2,)),
        ],
        input_output_aliases={6: 0},
        name="final",
    )(seq_lens, owner, query, arrived, mixed, stat, copied)

    every = lax.all_to_all(attention, "dp", split_axis=0, concat_axis=0, tiled=True)
    partial_sums = jnp.dot(
        every.reshape(devices * seqs, local_q * lanes),
        out_weight,
        preferred_element_type=jnp.float32,
    )
    summed = exchange_sum(partial_sums, tensor)
    return (new_pages.reshape(kv_pages.shape), summed)


def solution(mesh):
    placed = (
        P("dp", "tensor", None),
        P("dp", "tensor", None, None, None),
        P("dp", None, None),
        P("dp"),
        P("dp", None),
        P("dp"),
        P("tensor", "dp"),
    )
    return jax.shard_map(
        body,
        mesh=mesh,
        in_specs=placed,
        out_specs=(P("dp", "tensor", None, None, None), P(None, "dp")),
        check_vma=False,
    )
```

```python
import functools
import math

import jax
import jax.numpy as jnp
from jax import lax
from jax.experimental import pallas as pl
from jax.experimental.pallas import tpu as pltpu
from jax.sharding import PartitionSpec as P

CAP = 2
ROW = 8
NEG = -1e30

ANY = pl.BlockSpec(memory_space=pl.ANY)
VMEM = pl.BlockSpec(memory_space=pltpu.VMEM)
SMEM = pl.BlockSpec(memory_space=pltpu.SMEM)


def pack_kernel(plan_in, count_in, pages, out, plan, count, used, tags, sem, small_sem):
    devices = out.shape[0]
    rows = pages.shape[1]
    moves = plan.shape[2]
    small = [
        pltpu.make_async_copy(plan_in, plan, small_sem.at[0]),
        pltpu.make_async_copy(count_in, count, small_sem.at[1]),
    ]
    for copy in small:
        copy.start()
    for d in range(devices):
        used[d] = 0
        for r in range(CAP):
            tags[d * CAP + r] = -1
    for copy in small:
        copy.wait()

    def page_copy(source, target, rank):
        place = pl.ds(pl.multiple_of(rank * rows, rows), rows)
        return pltpu.make_async_copy(pages.at[source], out.at[target, place], sem)

    def send(k, carry):
        @pl.when(k < count[0])
        def _():
            target = plan[1, 0, k]
            rank = used[target]
            used[target] = rank + 1
            tags[target * CAP + rank] = plan[2, 0, k]
            page_copy(plan[0, 0, k], target, rank).start()

        return carry

    lax.fori_loop(0, moves, send, 0)
    row_at = lax.broadcasted_iota(jnp.int32, (ROW, pages.shape[2]), 0)
    for d in range(devices):
        tile = jnp.full(row_at.shape, -1, jnp.int32)
        for r in range(CAP):
            tile = jnp.where(row_at == r, tags[d * CAP + r], tile)
        out[d, CAP * rows :] = tile.astype(jnp.float32).astype(out.dtype)

    def finish(k, carry):
        @pl.when(k < count[0])
        def _():
            page_copy(0, 0, 0).wait()

        return carry

    lax.fori_loop(0, moves, finish, 0)


def partials(q_groups, key_pages, value_pages, firsts, lengths, scale):
    scores = [
        lax.dot_general(
            q, k, (((1,), (1,)), ((), ())), preferred_element_type=jnp.float32
        )
        * scale
        for q, k in zip(q_groups, key_pages)
    ]
    position = lax.broadcasted_iota(jnp.int32, scores[0].shape, 1)
    scores = jnp.stack(
        [
            jnp.where(position < length - first, s, NEG)
            for s, first, length in zip(scores, firsts, lengths)
        ]
    )
    largest = jnp.max(scores, axis=2, keepdims=True)
    expo = jnp.exp(scores - largest)
    total = jnp.sum(expo, axis=2, keepdims=True)
    weights = expo.astype(jnp.bfloat16)
    mixed = jnp.stack(
        [
            jnp.dot(weights[n], v, preferred_element_type=jnp.float32)
            for n, v in enumerate(value_pages)
        ]
    )
    return (
        jnp.broadcast_to(largest, mixed.shape),
        jnp.broadcast_to(total, mixed.shape),
        mixed,
    )


def local_kernel(
    heads, scale, table, lens, query, pages, new_pages, mixed_out, top_out, sum_out, owner,
    held, read_sem, write_sem,
):
    slots = pages.shape[0]
    block = pages.shape[1] // (2 * heads)
    seqs, blocks = table.shape
    group = query.shape[1] // heads

    def read(i):
        return pltpu.make_async_copy(pages.at[i], held.at[i], read_sem.at[i])

    def write(i):
        return pltpu.make_async_copy(held.at[i], new_pages.at[i], write_sem)

    def start_read(i, carry):
        read(i).start()
        owner[i] = -1
        return carry

    lax.fori_loop(0, slots, start_read, 0)

    def own(i, carry):
        for b in range(blocks):
            owner[table[i, b]] = i * blocks + b
        return carry

    lax.fori_loop(0, seqs, own, 0)

    def pass_on(i, carry):
        read(i).wait()
        write(i).start()
        return carry

    lax.fori_loop(0, slots, pass_on, 0)

    def sequence(i, carry):
        q_rows = query[i].astype(jnp.float32)
        places = [(b, h) for b in range(blocks) for h in range(heads)]
        groups = [
            q_rows[h * group : (h + 1) * group].astype(jnp.bfloat16) for h in range(heads)
        ]
        slot = [table[i, b] for b in range(blocks)]
        found = partials(
            [groups[h] for b, h in places],
            [held[slot[b], 2 * h * block : (2 * h + 1) * block] for b, h in places],
            [held[slot[b], (2 * h + 1) * block : (2 * h + 2) * block] for b, h in places],
            [b * block for b, h in places],
            [lens[i]] * len(places),
            scale,
        )
        for ref, value in zip((top_out, sum_out, mixed_out), found):
            ref[pl.ds(i * blocks, blocks)] = value.reshape(blocks, heads * group, -1)
        return carry

    lax.fori_loop(0, seqs, sequence, 0)

    def finish(i, carry):
        write(i).wait()
        return carry

    lax.fori_loop(0, slots, finish, 0)


def final_kernel(
    heads, scale, copies, lens, owner, query, arrived_in, mixed_in, top_in, sum_in, pages_in,
    pages_out, out, arrived, mixed, top, total, tags, sem, in_sem, tag_sem, page_sem,
):
    devices = arrived.shape[0]
    rows = pages_out.shape[1]
    block = rows // (2 * heads)
    seqs = query.shape[0]
    entries = mixed_in.shape[0]
    blocks = entries // seqs
    group = query.shape[1] // heads
    lanes = query.shape[2]
    tag_rows = pl.ds(CAP * rows, ROW)
    page_rows = pl.ds(0, CAP * rows)
    tag_copy = pltpu.make_async_copy(arrived_in.at[:, tag_rows], arrived.at[:, tag_rows], tag_sem)
    tag_copy.start()
    bring = [
        pltpu.make_async_copy(arrived_in.at[d, page_rows], arrived.at[d, page_rows], page_sem.at[d])
        for d in range(devices)
    ]
    for copy in bring:
        copy.start()
    fetch = [
        pltpu.make_async_copy(source, target.at[pl.ds(0, entries)], in_sem.at[n])
        for n, (source, target) in enumerate(((mixed_in, mixed), (top_in, top), (sum_in, total)))
    ]
    for copy in fetch:
        copy.start()

    tag_copy.wait()
    row_at = lax.broadcasted_iota(jnp.int32, (ROW, lanes), 0)
    for d in range(devices):
        tile = arrived[d, CAP * rows :].astype(jnp.float32)
        for r in range(CAP):
            tags[d * CAP + r] = jnp.max(jnp.where(row_at == r, tile, -1.0)).astype(jnp.int32)

    def place(d, r, slot):
        return pltpu.make_async_copy(
            arrived.at[d, pl.ds(r * rows, rows)], pages_out.at[slot], sem
        )

    for d in range(devices):
        bring[d].wait()
        for r in range(CAP):
            @pl.when(tags[d * CAP + r] >= 0)
            def _():
                place(d, r, tags[d * CAP + r]).start()

    for copy in fetch:
        copy.wait()

    def renew(sources):
        pairs = [(d, r) for d in sources for r in range(CAP)]
        q_groups, keys, values, firsts, lengths, targets = [], [], [], [], [], []
        for d, r in pairs:
            slot = tags[d * CAP + r]
            entry = jnp.where(slot >= 0, owner[jnp.maximum(slot, 0)], -1)
            at = jnp.maximum(entry, 0)
            i = at // blocks
            targets.append(jnp.where(entry >= 0, entry, entries))
            q_rows = query[i].astype(jnp.float32)
            for h in range(heads):
                q_groups.append(q_rows[h * group : (h + 1) * group].astype(jnp.bfloat16))
                start = r * rows + 2 * h * block
                keys.append(arrived[d, start : start + block])
                values.append(arrived[d, start + block : start + 2 * block])
                firsts.append((at - i * blocks) * block)
                lengths.append(lens[i])
        found = partials(q_groups, keys, values, firsts, lengths, scale)
        for ref, value in zip((top, total, mixed), found):
            pages_value = value.reshape(len(pairs), heads * group, lanes)
            for n, target in enumerate(targets):
                ref[target] = pages_value[n]

    if devices <= 8:
        renew(range(devices))
    else:
        lax.fori_loop(0, devices, lambda d, c: (renew([d]), c)[1], 0)

    for i in range(seqs):
        mine = pl.ds(i * blocks, blocks)
        largest = top[mine]
        factor = jnp.exp(largest - jnp.max(largest, axis=0, keepdims=True))
        value = jnp.sum(mixed[mine] * factor, axis=0) / jnp.sum(total[mine] * factor, axis=0)
        value = value.astype(out.dtype)
        for c in range(copies):
            out[c, i] = value

    for d in range(devices):
        for r in range(CAP):
            @pl.when(tags[d * CAP + r] >= 0)
            def _():
                place(d, r, 0).wait()


def exchange_sum(value, size):
    me = lax.axis_index("tensor")
    pairs = lambda bit: [(i, i ^ bit) for i in range(size)]
    half = value.shape[0] // 2
    low = (me % 2) == 0
    travel = value.astype(jnp.bfloat16)
    given = jnp.where(low, travel[half:], travel[:half])
    kept = jnp.where(low, value[:half], value[half:])
    total = kept + lax.ppermute(given, "tensor", pairs(1)).astype(jnp.float32)
    bit = 2
    while bit < size:
        total = total + lax.ppermute(
            total.astype(jnp.bfloat16), "tensor", pairs(bit)
        ).astype(jnp.float32)
        bit *= 2
    mine = total.astype(jnp.bfloat16)
    other = lax.ppermute(mine, "tensor", pairs(1))
    return jnp.concatenate([jnp.where(low, mine, other), jnp.where(low, other, mine)])


def body(query, kv_pages, move_plan, move_count, block_table, seq_lens, out_weight):
    slots, heads, two, block, lanes = kv_pages.shape
    seqs, local_q, _ = query.shape
    devices = lax.axis_size("dp")
    tensor = lax.axis_size("tensor")
    blocks = block_table.shape[1]
    group = local_q // heads
    rows = heads * two * block
    scale = 1.0 / math.sqrt(lanes)
    pages = kv_pages.reshape(slots, rows, lanes)
    plan = jnp.transpose(move_plan, (1, 0, 2))

    outgoing = pl.pallas_call(
        pack_kernel,
        out_shape=jax.ShapeDtypeStruct((devices, CAP * rows + ROW, lanes), kv_pages.dtype),
        in_specs=[ANY, ANY, ANY],
        out_specs=VMEM,
        scratch_shapes=[
            pltpu.SMEM(plan.shape, jnp.int32),
            pltpu.SMEM((1,), jnp.int32),
            pltpu.SMEM((devices,), jnp.int32),
            pltpu.SMEM((devices * CAP,), jnp.int32),
            pltpu.SemaphoreType.DMA,
            pltpu.SemaphoreType.DMA((2,)),
        ],
        name="pack",
    )(plan, move_count, pages)
    arrived = lax.all_to_all(outgoing, "dp", split_axis=0, concat_axis=0, tiled=True)

    entries = seqs * blocks
    part_shape = jax.ShapeDtypeStruct((entries, local_q, lanes), jnp.float32)
    part_scratch = pltpu.VMEM((entries + 1, local_q, lanes), jnp.float32)
    copied, mixed, top, total, owner = pl.pallas_call(
        functools.partial(local_kernel, heads, scale),
        out_shape=(
            jax.ShapeDtypeStruct(pages.shape, pages.dtype),
            part_shape,
            part_shape,
            part_shape,
            jax.ShapeDtypeStruct((slots,), jnp.int32),
        ),
        in_specs=[SMEM, SMEM, VMEM, ANY],
        out_specs=(ANY, VMEM, VMEM, VMEM, SMEM),
        scratch_shapes=[
            pltpu.VMEM(pages.shape, pages.dtype),
            pltpu.SemaphoreType.DMA((slots,)),
            pltpu.SemaphoreType.DMA,
        ],
        name="local",
        cost_estimate=pl.CostEstimate(
            flops=4 * seqs * blocks * local_q * block * lanes,
            bytes_accessed=4 * slots * rows * lanes,
            transcendentals=0,
        ),
        compiler_params=pltpu.CompilerParams(vmem_limit_bytes=24 << 20),
    )(block_table, seq_lens, query, pages)

    new_pages, attention = pl.pallas_call(
        functools.partial(final_kernel, heads, scale, devices),
        out_shape=(
            jax.ShapeDtypeStruct(pages.shape, pages.dtype),
            jax.ShapeDtypeStruct((devices, seqs, local_q, lanes), jnp.bfloat16),
        ),
        in_specs=[SMEM, SMEM, VMEM, ANY, ANY, ANY, ANY, ANY],
        out_specs=(ANY, VMEM),
        scratch_shapes=[
            pltpu.VMEM(arrived.shape, arrived.dtype),
            part_scratch,
            part_scratch,
            part_scratch,
            pltpu.SMEM((devices * CAP,), jnp.int32),
            pltpu.SemaphoreType.DMA,
            pltpu.SemaphoreType.DMA((3,)),
            pltpu.SemaphoreType.DMA,
            pltpu.SemaphoreType.DMA((devices,)),
        ],
        input_output_aliases={7: 0},
        name="final",
        compiler_params=pltpu.CompilerParams(vmem_limit_bytes=24 << 20),
    )(seq_lens, owner, query, arrived, mixed, top, total, copied)

    every = lax.all_to_all(attention, "dp", split_axis=0, concat_axis=0, tiled=True)
    partial_sums = jnp.dot(
        every.reshape(devices * seqs, local_q * lanes),
        out_weight,
        preferred_element_type=jnp.float32,
    )
    summed = exchange_sum(partial_sums, tensor)
    return (new_pages.reshape(kv_pages.shape), summed)


def solution(mesh):
    placed = (
        P("dp", "tensor", None),
        P("dp", "tensor", None, None, None),
        P("dp", None, None),
        P("dp"),
        P("dp", None),
        P("dp"),
        P("tensor", "dp"),
    )
    return jax.shard_map(
        body,
        mesh=mesh,
        in_specs=placed,
        out_specs=(P("dp", "tensor", None, None, None), P(None, "dp")),
        check_vma=False,
    )
```
